32 devices in a mesh: section: 2 (over x), dp: 4 (over z), mp: 4 (over y, core).
Axes of the slice: x: 2, y: 2, z: 4, core: 2. Of those that a mesh axis runs over, the one named last changes fastest.
Arguments:
- w_query: bfloat16 [2, 4096, 4096], P('section', None, 'mp'), may hold values from -0.09375 to 0.09375
- w_key: bfloat16 [2, 4096, 1024], P('section', None, 'mp'), may hold values from -0.09375 to 0.09375
- w_value: bfloat16 [2, 4096, 1024], P('section', None, 'mp'), may hold values from -0.09375 to 0.09375
- w_out: bfloat16 [2, 4096, 4096], P('section', 'mp'), may hold values from -0.09375 to 0.09375
- norm_gain: bfloat16 [2, 4096], P('section', 'mp'), may hold values from 0.099609375 to 1.8984375
- saved_input: bfloat16 [2, 2, 4, 64, 4096], P('section', None, 'dp', None, 'mp'), may hold values from -6 to 6
- saved_query: bfloat16 [2, 2, 4, 64, 4096], P('section', None, 'dp', None, 'mp'), may hold values from -5 to 5
- saved_key: bfloat16 [2, 2, 4, 64, 1024], P('section', None, 'dp', None, 'mp'), may hold values from -5 to 5
- saved_value: bfloat16 [2, 2, 4, 64, 1024], P('section', None, 'dp', None, 'mp'), may hold values from -6 to 6
- grad_in: bfloat16 [2, 4, 64, 4096], P('section', 'dp', None, 'mp'), may hold values from -0.29882812 to 0.29882812
- fresh_grad: bfloat16 [1, 4, 64, 4096], P(None, 'dp', None, 'mp'), may hold values from -0.29882812 to 0.29882812
- features: bfloat16 [2, 4, 16, 7680], P(None, 'dp', None, 'section'), may hold values from -6 to 6
- image_pos: int32 [2, 4, 16], P(None, 'dp'), may hold values from 0 to 63, as said below
Outputs:
- proj_grad: bfloat16 [7680, 4096], P(('section', 'dp'), 'mp')
- pending: bfloat16 [2, 4, 64, 4096], P('section', 'dp', None, 'mp')
The draws below stay inside these ranges and needn't reach their ends.
Inputs may be any that keep to these rules, and one draw needn't show every extreme that they name: `image_pos`: each row holds 16 consecutive ascending positions; the first row starts at 0 and the last ends at 63.
All inputs are finite; a program needn't handle non-finite values.
Results may differ from the reference program's by a relative error of at most 0.017.
Values may be sent and summed in bfloat16 or wider, within the bound.
A program may use at most 64 MiB of HBM per device.

```python
import jax
import jax.numpy as jnp
from jax import lax

D = 4096
HEADS = 32
KVH = 8
HD = 128
VF = 7680
L = 64
IMG = 16
TICKS = 2
QW = 4096
KW = 1024
NSEQ = 4
N_SECTION = 2
N_MP = 4


def score_pair(key):
    keys = jax.random.split(jax.random.fold_in(key, 7), 2)
    group = HEADS // KVH
    key_arr = jnp.clip(jax.random.normal(keys[0], (N_SECTION, TICKS, NSEQ, L, KVH, HD), jnp.float32), -5.0, 5.0)
    query_arr = jnp.clip(jax.random.normal(keys[1], (N_SECTION, TICKS, NSEQ, L, KVH, group, HD), jnp.float32), -5.0, 5.0)
    return (query_arr.reshape(N_SECTION, TICKS, NSEQ, L, HEADS * HD), key_arr.reshape(N_SECTION, TICKS, NSEQ, L, KVH * HD))


def draw_saved_query(key, part):
    return score_pair(key)[0].astype(jnp.bfloat16)


def draw_saved_key(key, part):
    return score_pair(key)[1].astype(jnp.bfloat16)


def draw_image_pos(key, part):
    count = TICKS * NSEQ
    starts = jax.random.randint(jax.random.fold_in(key, 3), (count,), 0, L - IMG + 1)
    starts = starts.at[0].set(0).at[count - 1].set(L - IMG)
    starts = starts.reshape(TICKS, NSEQ)
    return (starts[:, :, None] + jnp.arange(IMG)[None, None, :]).astype(jnp.int32)


def levels(key, extent, shards, low, top_value):
    def one(axis_at, blocks):
        draws = jax.random.uniform(jax.random.fold_in(jax.random.fold_in(key, 6), axis_at), (blocks,), jnp.float32, low / len(shards), top_value / len(shards))
        return jnp.repeat(jnp.exp(draws), extent[axis_at] // blocks).reshape((-1,) + (1,) * (len(extent) - axis_at - 1))

    factor_of = one(*shards[0])
    for cut in shards[1:]:
        factor_of = factor_of * one(*cut)
    return factor_of


def centred(own_key, dims, deviation, bound, pieces=(), held_as=jnp.bfloat16):
    level = levels(own_key, dims, pieces, -0.22, 0.18) if pieces else 1.0
    entries = jax.random.normal(own_key, dims, jnp.float32) * deviation * level
    return jnp.minimum(jnp.maximum(entries, -bound), bound).astype(held_as)


def setup_inputs(seed: int = 0) -> dict:
    key_of = jax.random.split(jax.random.key(seed), 14)
    w_query = centred(key_of[0], (N_SECTION, D, QW), D ** -0.5, 0.09375, ((0, 2), (2, 4)))
    w_key = centred(key_of[1], (N_SECTION, D, KW), D ** -0.5, 0.09375, ((0, 2), (2, 4)))
    w_value = centred(key_of[2], (N_SECTION, D, KW), D ** -0.5, 0.09375, ((0, 2), (2, 4)))
    w_out = centred(key_of[3], (N_SECTION, QW, D), QW ** -0.5, 0.09375, ((0, 2), (1, 4)))
    norm_gain = jnp.clip(1.0 + 0.18 * jax.random.normal(key_of[4], (N_SECTION, D), jnp.float32), 0.099609375, 1.8984375).astype(jnp.bfloat16)
    saved_input = centred(key_of[5], (N_SECTION, TICKS, NSEQ, L, D), 1.0, 6.0, ((0, 2), (2, 4), (4, 4)))
    saved_query = draw_saved_query(jax.random.fold_in(key_of[13], 71), 0)
    saved_key = draw_saved_key(jax.random.fold_in(key_of[13], 71), 0)
    saved_value = centred(key_of[8], (N_SECTION, TICKS, NSEQ, L, KW), 1.0, 6.0, ((0, 2), (2, 4), (4, 4)))
    grad_in = centred(key_of[9], (N_SECTION, NSEQ, L, D), 0.05, 0.29882812, ((0, 2), (1, 4), (3, 4)))
    fresh_grad = centred(key_of[10], (TICKS - 1, NSEQ, L, D), 0.05, 0.29882812, ((1, 4), (3, 4)))
    features = centred(key_of[11], (TICKS, NSEQ, IMG, VF), 1.0, 6.0, ((1, 4), (3, 2)))
    image_pos = draw_image_pos(jax.random.fold_in(key_of[13], 71), 0)
    return {"w_query": w_query, "w_key": w_key, "w_value": w_value, "w_out": w_out, "norm_gain": norm_gain, "saved_input": saved_input, "saved_query": saved_query, "saved_key": saved_key, "saved_value": saved_value, "grad_in": grad_in, "fresh_grad": fresh_grad, "features": features, "image_pos": image_pos}


def to_half(value):
    return lax.optimization_barrier(value.astype(jnp.bfloat16)).astype(jnp.float32)

def segment_back(grad, x_saved, gain, w_q, w_k, w_v, w_o, query, key_in, value):
    seq_len = grad.shape[0]
    group = HEADS // KVH
    scale = HD ** (-0.5)
    d_attn = jnp.dot(grad, w_o.T, preferred_element_type=jnp.float32).astype(jnp.bfloat16)
    q_four = query.astype(jnp.float32).reshape(seq_len, KVH, group, HD)
    k_three = key_in.astype(jnp.float32).reshape(seq_len, KVH, HD)
    v_three = value.astype(jnp.float32).reshape(seq_len, KVH, HD)
    a_four = d_attn.astype(jnp.float32).reshape(seq_len, KVH, group, HD)
    scores = jnp.einsum('lgjd,mgd->gjlm', q_four, k_three) * scale
    rows = jnp.arange(seq_len)[:, None]
    cols = jnp.arange(seq_len)[None, :]
    scores = jnp.where(cols <= rows, scores, -1e+30)
    top = lax.optimization_barrier(jnp.max(scores, -1, keepdims=True))
    expo = jnp.exp(scores - top)
    probs = expo / lax.optimization_barrier(jnp.sum(expo, -1, keepdims=True))
    d_probs = jnp.einsum('lgjd,mgd->gjlm', a_four, v_three)
    inner = lax.optimization_barrier(jnp.sum(probs * d_probs, -1, keepdims=True))
    d_scores = to_half(probs * (d_probs - inner) * scale)
    probs_half = to_half(probs)
    d_query = jnp.einsum('gjlm,mgd->lgjd', d_scores, k_three).astype(jnp.bfloat16).reshape(seq_len, QW)
    d_key = jnp.einsum('gjlm,lgjd->mgd', d_scores, q_four).astype(jnp.bfloat16).reshape(seq_len, KW)
    d_value = jnp.einsum('gjlm,lgjd->mgd', probs_half, a_four).astype(jnp.bfloat16).reshape(seq_len, KW)
    parts = N_MP
    term = jnp.einsum('lnc,dnc->nld', d_query.astype(jnp.float32).reshape(seq_len, parts, QW // parts), w_q.astype(jnp.float32).reshape(D, parts, QW // parts))
    term = term + jnp.einsum('lnc,dnc->nld', d_key.astype(jnp.float32).reshape(seq_len, parts, KW // parts), w_k.astype(jnp.float32).reshape(D, parts, KW // parts))
    term = term + jnp.einsum('lnc,dnc->nld', d_value.astype(jnp.float32).reshape(seq_len, parts, KW // parts), w_v.astype(jnp.float32).reshape(D, parts, KW // parts))
    d_normed = lax.optimization_barrier(jnp.sum(to_half(term), axis=0))
    x_float = x_saved.astype(jnp.float32)
    rstd = lax.rsqrt(lax.optimization_barrier(jnp.mean(x_float * x_float, -1, keepdims=True)) + 1e-05)
    weighted = gain.astype(jnp.float32) * d_normed
    cross = lax.optimization_barrier(jnp.mean(x_float * weighted, -1, keepdims=True))
    d_input = rstd * weighted - x_float * rstd ** 3 * cross
    return (grad.astype(jnp.float32) + d_input).astype(jnp.bfloat16)

def reference(w_query, w_key, w_value, w_out, norm_gain, saved_input, saved_query, saved_key, saved_value, grad_in, fresh_grad, features, image_pos):
    per_seq = jax.vmap(segment_back, in_axes=(0, 0, None, None, None, None, None, 0, 0, 0))

    def one_layer(layer):
        grad, x_saved, gain, w_q, w_k, w_v, w_o, query, key_in, value = layer
        return per_seq(grad, x_saved, gain, w_q, w_k, w_v, w_o, query, key_in, value)

    def run_tick(grads, tick):
        return lax.map(one_layer, (grads, saved_input[:, tick], norm_gain, w_query, w_key, w_value, w_out, saved_query[:, tick], saved_key[:, tick], saved_value[:, tick]))
    produced = run_tick(grad_in, 0)
    total = jnp.zeros((VF, D), jnp.float32)
    for tick in range(TICKS):
        if tick > 0:
            incoming = jnp.concatenate([produced[1:], fresh_grad[tick - 1][None]], axis=0)
            produced = run_tick(incoming, tick)
        picked = jnp.take_along_axis(produced[0], image_pos[tick].astype(jnp.int32)[:, :, None], axis=1)
        total = total + jnp.einsum('nif,nid->fd', features[tick].astype(jnp.float32), picked.astype(jnp.float32))
    return (total.astype(jnp.bfloat16), produced)
```

```python
import functools

import jax
import jax.numpy as jnp
from jax import lax
from jax.experimental import pallas as pl
from jax.experimental.pallas import tpu as pltpu
from jax.sharding import PartitionSpec as P

HD = 128
LANES = 128
TICKS = 2
GAIN_ROWS = 16
MESH = pl.DeviceIdType.MESH
LAST = (((1,), (1,)), ((), ()))
FIRST = (((0,), (0,)), ((), ()))
PLAIN = (((1,), (0,)), ((), ()))


def mul(a, b, dims):
    return lax.dot_general(a, b, dims, preferred_element_type=jnp.float32)


def lane_sum(a):
    parts = [a[:, i : i + LANES] for i in range(0, a.shape[1], LANES)]
    return functools.reduce(lambda p, q: p + q, parts)


def kernel(
    n_section, n_dp, n_mp, pieces,
    wq, wk, wv, wo, gain, x, q, k, v, g_in, fresh, feat, pos,
    feat_all, picks, pending,
    wq_s, wk_s, wv_s, wo_s, gain_s, x_s, q_s, k_s, v_s, g_s, feat_s, cut_s, pos_s,
    probs_s, attn_s, dq_s, dk_s, dv_s, out_s, send_s, recv_s, cross_s, cross_r,
    load_sem, wo_sem, wq_sem, wk_sem, wv_sem,
    ag_send, ag_recv, xg_send, xg_recv, rs_send, rs_recv, cr_send, cr_recv,
    held_send, held_recv, ft_send, ft_recv, px_send, px_recv, pz_send, pz_recv,
):
    section = lax.axis_index("section")
    seq = lax.axis_index("dp")
    me = lax.axis_index("mp")
    y, core = me // 2, me % 2
    partner = 2 * y + (1 - core)
    across = 2 * (1 - y) + core
    diag = 2 * (1 - y) + (1 - core)
    length = g_in.shape[2]
    width = g_in.shape[3]
    depth = width * n_mp
    kv_local = k.shape[4] // HD
    group = q.shape[4] // k.shape[4]
    scale = HD ** (-0.5)
    f32, bf16 = jnp.float32, jnp.bfloat16

    def remote(src, dst, ssem, rsem, where):
        return pltpu.make_async_remote_copy(
            src_ref=src, dst_ref=dst, send_sem=ssem, recv_sem=rsem,
            device_id=where, device_id_type=MESH,
        )

    loads = {}

    def load(name, src, dst, sem):
        loads[name] = pltpu.make_async_copy(src, dst, sem)
        loads[name].start()

    load("g", g_in.at[0, 0], g_s.at[0, me], load_sem.at[0])
    load("x0", x.at[0, 0, 0], x_s.at[0, me, pl.ds(0, length)], load_sem.at[1])
    load("gain", gain, gain_s, load_sem.at[2])
    load("x1", x.at[0, 1, 0], x_s.at[1, me, pl.ds(0, length)], load_sem.at[3])
    load("q", q.at[0, :, 0], q_s, load_sem.at[4])
    load("k", k.at[0, :, 0], k_s, load_sem.at[5])
    load("v", v.at[0, :, 0], v_s, load_sem.at[6])
    load("feat", feat.at[:, 0], feat_s, load_sem.at[7])
    load("pos", pos.at[:, 0], pos_s, load_sem.at[8])
    order = (me, partner, across, diag)
    for i, b in enumerate(order):
        columns = pl.ds(pl.multiple_of(b * width, width), width)
        load(f"wo{i}", wo.at[0, :, columns], wo_s.at[b], wo_sem.at[i])
    for i, b in enumerate((diag, across, partner, me)):
        rows = pl.ds(pl.multiple_of(b * width, width), width)
        load(f"wk{i}", wk.at[0, rows], wk_s.at[b], wk_sem.at[i])
        load(f"wv{i}", wv.at[0, rows], wv_s.at[b], wv_sem.at[i])
        load(f"wq{i}", wq.at[0, rows], wq_s.at[b], wq_sem.at[i])

    barrier = pltpu.get_barrier_semaphore()
    for b in (partner, across, diag):
        pl.semaphore_signal(barrier, inc=1, device_id={"mp": b}, device_id_type=MESH)
    for o in range(1, n_dp):
        pl.semaphore_signal(
            barrier, inc=1, device_id={"dp": (seq + o) % n_dp}, device_id_type=MESH
        )
    for o in range(1, n_section):
        pl.semaphore_signal(
            barrier, inc=1, device_id={"section": (section + o) % n_section}, device_id_type=MESH
        )
    pl.semaphore_wait(barrier, 3 + n_dp - 1 + n_section - 1)

    def gather_copy(buf, slot, rows, ssem, rsem, where):
        ref = buf.at[slot, rows]
        return remote(ref, ref, ssem, rsem, {"mp": where})

    def gather_start(buf, rows, ssem, rsem):
        gather_copy(buf, me, rows, ssem.at[1], rsem.at[1], across).start()
        gather_copy(buf, me, rows, ssem.at[0], rsem.at[0], partner).start()

    def gather_forward(buf, rows, ssem, rsem):
        gather_copy(buf, across, rows, ssem.at[1], rsem.at[1], across).wait_recv()
        gather_copy(buf, across, rows, ssem.at[2], rsem.at[2], partner).start()

    def gather_wait(buf, slot, which, rows, ssem, rsem):
        gather_copy(buf, slot, rows, ssem.at[which], rsem.at[which], partner).wait_recv()

    def gather_drain(buf, rows, ssem, rsem):
        for i in range(3):
            gather_copy(buf, me, rows, ssem.at[i], rsem.at[i], partner).wait_send()

    full = pl.ds(0, length)
    x_rows = (pl.ds(0, length + GAIN_ROWS), pl.ds(0, length))
    loads["g"].wait()
    gather_start(g_s.at[0], full, ag_send.at[0, 0], ag_recv.at[0, 0])
    loads["x0"].wait()
    loads["gain"].wait()
    x_s[0, me, pl.ds(length, GAIN_ROWS), :] = jnp.broadcast_to(
        gain_s[...], (GAIN_ROWS, width)
    )
    gather_start(x_s.at[0], x_rows[0], xg_send.at[0], xg_recv.at[0])
    loads["x1"].wait()
    gather_start(x_s.at[1], x_rows[1], xg_send.at[1], xg_recv.at[1])

    loads["feat"].wait()
    own_rows = feat_s.shape[2] // n_dp
    for j in range(n_dp):
        for t in range(TICKS):
            cut_s[j, pl.ds(t * feat_s.shape[1], feat_s.shape[1]), :] = feat_s[
                t, :, j * own_rows : (j + 1) * own_rows
            ]
    feat_own = pltpu.make_async_copy(cut_s.at[seq], feat_all.at[seq], load_sem.at[9])
    feat_own.start()

    def feat_copy(o):
        to = (seq + o) % n_dp
        return remote(
            cut_s.at[to], feat_all.at[seq], ft_send.at[o], ft_recv.at[o], {"dp": to}
        )

    for o in range(1, n_dp):
        feat_copy(o).start()

    loads["q"].wait()
    loads["k"].wait()
    loads["v"].wait()

    def stack(a, g):
        return jnp.concatenate(
            [a[:, (g * group + j) * HD : (g * group + j + 1) * HD] for j in range(group)], axis=0
        )

    rows_at = lax.rem(
        lax.broadcasted_iota(jnp.int32, (group * length, length), 0), jnp.int32(length)
    )
    cols_at = lax.broadcasted_iota(jnp.int32, (group * length, length), 1)
    causal = cols_at <= rows_at

    def softmax(t):
        for g in range(kv_local):
            kg = k_s[t, :, g * HD : (g + 1) * HD]
            scores = mul(stack(q_s[t], g), kg, LAST) * scale
            scores = jnp.where(causal, scores, -1e30)
            expo = jnp.exp(scores - jnp.max(scores, -1, keepdims=True))
            probs_s[t, g] = expo / jnp.sum(expo, -1, keepdims=True)

    for t in range(TICKS):
        softmax(t)

    def picks_second(t):
        @pl.when(section > 0)
        def _():
            remote(
                picks.at[seq, t], picks.at[seq, t], px_send.at[t, 0], px_recv.at[t],
                {"section": section},
            ).wait_recv()

        for o in range(1, n_dp):
            pick_copy(t, o).start()

    def pick_copy(t, o):
        to = (seq + o) % n_dp
        ref = picks.at[seq, t]
        return remote(ref, ref, pz_send.at[t, o], pz_recv.at[t, o], {"dp": to})

    def pick_spread(t, o):
        ref = picks.at[seq, t]
        return remote(ref, ref, px_send.at[t, o], px_recv.at[t], {"section": o})

    def rs_copy(t, i, where):
        return remote(
            send_s.at[t, i], recv_s.at[t, i], rs_send.at[t, i], rs_recv.at[t, i], {"mp": where}
        )

    def cross_copy(t, i, where):
        return remote(
            cross_s.at[t], cross_r.at[t, i], cr_send.at[t, i], cr_recv.at[t, i], {"mp": where}
        )

    part = length // pieces

    def held_copy(h):
        rows = pl.ds(h * part, part)
        return remote(
            out_s.at[0, rows], g_s.at[1, me, rows], held_send.at[h], held_recv.at[h],
            {"section": section - 1},
        )

    def finish_gather(t, rows_list):
        for h, rows in enumerate(rows_list):
            gather_forward(g_s.at[t], rows, ag_send.at[t, h], ag_recv.at[t, h])

    def tick(t):
        rows_list = [full] if t == 0 else [pl.ds(h * part, part) for h in range(pieces)]
        first = t == 0
        if t == 1:

            @pl.when(section == n_section - 1)
            def _():
                fresh_copy = pltpu.make_async_copy(
                    fresh.at[0, 0], g_s.at[1, me], load_sem.at[10]
                )
                fresh_copy.start()
                fresh_copy.wait()

            for h, rows in enumerate(rows_list):

                @pl.when(section < n_section - 1)
                def _():
                    held_copy(h).wait_recv()

                gather_start(g_s.at[1], rows, ag_send.at[1, h], ag_recv.at[1, h])
        if first:
            loads["wo0"].wait()
        d_attn = mul(g_s[t, me], wo_s[me], LAST)
        for h, rows in enumerate(rows_list):
            gather_wait(g_s.at[t], partner, 0, rows, ag_send.at[t, h], ag_recv.at[t, h])
        if first:
            loads["wo1"].wait()
        d_attn += mul(g_s[t, partner], wo_s[partner], LAST)
        finish_gather(t, rows_list)
        if first:
            loads["wo2"].wait()
        d_attn += mul(g_s[t, across], wo_s[across], LAST)
        for h, rows in enumerate(rows_list):
            gather_wait(g_s.at[t], diag, 2, rows, ag_send.at[t, h], ag_recv.at[t, h])
        if first:
            loads["wo3"].wait()
        d_attn += mul(g_s[t, diag], wo_s[diag], LAST)
        attn_s[...] = d_attn.astype(bf16)
        if first:
            gather_forward(x_s.at[0], x_rows[0], xg_send.at[0], xg_recv.at[0])
        else:
            picks_second(0)

        for g in range(kv_local):
            lanes = slice(g * HD, (g + 1) * HD)
            kg, vg = k_s[t, :, lanes], v_s[t, :, lanes]
            qg = stack(q_s[t], g)
            ag = stack(attn_s[...], g)
            probs = probs_s[t, g]
            d_probs = mul(ag, vg, LAST)
            inner = jnp.sum(probs * d_probs, -1, keepdims=True)
            d_scores = (probs * (d_probs - inner) * scale).astype(bf16)
            d_query = mul(d_scores, kg, PLAIN).astype(bf16)
            for j in range(group):
                dq_s[:, (g * group + j) * HD : (g * group + j + 1) * HD] = d_query[
                    j * length : (j + 1) * length
                ]
            dk_s[:, lanes] = mul(d_scores, qg, FIRST).astype(bf16)
            dv_s[:, lanes] = mul(probs.astype(bf16), ag, FIRST).astype(bf16)

        if first:
            gather_wait(x_s.at[0], partner, 0, x_rows[0], xg_send.at[0], xg_recv.at[0])
            gather_wait(x_s.at[0], diag, 2, x_rows[0], xg_send.at[0], xg_recv.at[0])
        else:
            gather_wait(x_s.at[1], partner, 0, x_rows[1], xg_send.at[1], xg_recv.at[1])
            gather_wait(x_s.at[1], diag, 2, x_rows[1], xg_send.at[1], xg_recv.at[1])

        def x_of(b):
            return x_s[t, b, pl.ds(0, length), :].astype(f32)

        def gain_of(b):
            return x_s[0, b, pl.ds(length, GAIN_ROWS), :].astype(f32)[0:1]

        def partial(i, b):
            if first:
                loads[f"wk{i}"].wait()
                loads[f"wv{i}"].wait()
                loads[f"wq{i}"].wait()
            term = mul(dq_s[...], wq_s[b], LAST)
            term += mul(dk_s[...], wk_s[b], LAST)
            return term + mul(dv_s[...], wv_s[b], LAST)

        term = partial(0, diag)
        send_s[t, 0] = term.astype(bf16)
        rs_copy(t, 0, partner).start()
        total = lane_sum(x_of(diag) * gain_of(diag) * term)
        term = partial(1, across)
        rs_copy(t, 0, partner).wait_recv()
        send_s[t, 1] = (term + recv_s[t, 0].astype(f32)).astype(bf16)
        rs_copy(t, 1, across).start()
        total += lane_sum(x_of(across) * gain_of(across) * term)
        term = partial(2, partner)
        send_s[t, 2] = term.astype(bf16)
        rs_copy(t, 2, partner).start()
        total += lane_sum(x_of(partner) * gain_of(partner) * term)
        term = partial(3, me)
        total += lane_sum(x_of(me) * gain_of(me) * term)
        padded = jnp.concatenate([total, jnp.zeros((LANES - length, LANES), f32)], axis=0)
        cross_s[t] = jnp.broadcast_to(
            jnp.sum(padded.T, axis=0, keepdims=True), cross_s.shape[1:]
        )
        for i, b in enumerate((partner, across, diag)):
            cross_copy(t, i, b).start()
        if first:
            gather_forward(x_s.at[1], x_rows[1], xg_send.at[1], xg_recv.at[1])
        squares = functools.reduce(
            lambda a, b: a + b, [lane_sum(x_of(b) * x_of(b)) for b in range(n_mp)]
        )
        squares = jnp.sum(squares, -1, keepdims=True)
        rstd = lax.rsqrt(squares / depth + 1e-05)
        rs_copy(t, 2, partner).wait_recv()
        term += recv_s[t, 2].astype(f32)
        rs_copy(t, 1, across).wait_recv()
        weighted = gain_of(me) * (term + recv_s[t, 1].astype(f32))
        cross = cross_s[t]
        for i in range(3):
            cross_copy(t, i, partner).wait_recv()
            cross += cross_r[t, i]
        cross = jnp.broadcast_to(cross[0:1], (LANES, LANES)).T[:length, 0:1]
        d_input = rstd * weighted - x_of(me) * (rstd * rstd * rstd) * (cross / depth)
        out_s[t] = (g_s[t, me].astype(f32) + d_input).astype(bf16)
        if first:

            @pl.when(section > 0)
            def _():
                for h in range(pieces):
                    held_copy(h).start()

            loads["pos"].wait()

        @pl.when(section == 0)
        def _():
            at = lax.broadcasted_iota(jnp.int32, (length, pos_s.shape[1]), 0)
            chosen = (at == pos_s[pl.ds(t, 1), :]).astype(f32).astype(bf16)
            picks[seq, t] = mul(chosen, out_s[t], FIRST).astype(bf16)
            for o in range(1, n_section):
                pick_spread(t, o).start()

    tick(0)
    tick(1)
    picks_second(1)
    pending[0, 0] = out_s[1]

    feat_own.wait()
    gather_drain(g_s.at[0], full, ag_send.at[0, 0], ag_recv.at[0, 0])
    for h in range(pieces):
        gather_drain(
            g_s.at[1], pl.ds(h * part, part), ag_send.at[1, h], ag_recv.at[1, h]
        )
    for t in range(TICKS):
        gather_drain(x_s.at[t], x_rows[t], xg_send.at[t], xg_recv.at[t])
        for i in range(3):
            rs_copy(t, i, partner).wait_send()
            cross_copy(t, i, partner).wait_send()

    @pl.when(section > 0)
    def _():
        for h in range(pieces):
            held_copy(h).wait_send()

    @pl.when(section == 0)
    def _():
        for t in range(TICKS):
            for o in range(1, n_section):
                pick_spread(t, o).wait_send()

    for o in range(1, n_dp):
        feat_copy(o).wait_send()
        source = (seq + n_dp - o) % n_dp
        remote(
            cut_s.at[seq], feat_all.at[source], ft_send.at[o], ft_recv.at[o], {"dp": source}
        ).wait_recv()
        for t in range(TICKS):
            pick_copy(t, o).wait_send()
            ref = picks.at[source, t]
            remote(ref, ref, pz_send.at[t, o], pz_recv.at[t, o], {"dp": source}).wait_recv()


def shards(
    w_query, w_key, w_value, w_out, norm_gain, saved_input, saved_query, saved_key,
    saved_value, grad_in, fresh_grad, features, image_pos, pieces=2,
):
    n_section, n_dp, n_mp = (lax.axis_size(a) for a in ("section", "dp", "mp"))
    assert n_mp == 4
    length, width = grad_in.shape[2:]
    kw = saved_key.shape[4]
    kv_local = kw // HD
    group = width // kw
    images = features.shape[2]
    own_rows = features.shape[3] // n_dp
    f32, bf16 = jnp.float32, jnp.bfloat16
    vmem, dma = pltpu.VMEM, pltpu.SemaphoreType.DMA
    feat_all, picks, pending = pl.pallas_call(
        functools.partial(kernel, n_section, n_dp, n_mp, pieces),
        out_shape=(
            jax.ShapeDtypeStruct((n_dp, TICKS * images, own_rows), bf16),
            jax.ShapeDtypeStruct((n_dp, TICKS, images, width), bf16),
            jax.ShapeDtypeStruct((1, 1, length, width), bf16),
        ),
        in_specs=[pl.BlockSpec(memory_space=pl.ANY)] * 13,
        out_specs=(pl.BlockSpec(memory_space=pltpu.VMEM),) * 3,
        scratch_shapes=[
            vmem((n_mp, width, width), bf16),
            vmem((n_mp, width, kw), bf16),
            vmem((n_mp, width, kw), bf16),
            vmem((n_mp, width, width), bf16),
            vmem((1, width), bf16),
            vmem((TICKS, n_mp, length + GAIN_ROWS, width), bf16),
            vmem((TICKS, length, width), bf16),
            vmem((TICKS, length, kw), bf16),
            vmem((TICKS, length, kw), bf16),
            vmem((TICKS, n_mp, length, width), bf16),
            vmem((TICKS, images, features.shape[3]), bf16),
            vmem((n_dp, TICKS * images, own_rows), bf16),
            vmem((TICKS, images), jnp.int32),
            vmem((TICKS, kv_local, group * length, length), f32),
            vmem((length, width), bf16),
            vmem((length, width), bf16),
            vmem((length, kw), bf16),
            vmem((length, kw), bf16),
            vmem((TICKS, length, width), bf16),
            vmem((TICKS, 3, length, width), bf16),
            vmem((TICKS, 3, length, width), bf16),
            vmem((TICKS, 8, LANES), f32),
            vmem((TICKS, 3, 8, LANES), f32),
            dma((11,)), dma((n_mp,)), dma((n_mp,)), dma((n_mp,)), dma((n_mp,)),
            dma((TICKS, pieces, 3)), dma((TICKS, pieces, 3)),
            dma((TICKS, 3)), dma((TICKS, 3)),
            dma((TICKS, 3)), dma((TICKS, 3)), dma((TICKS, 3)), dma((TICKS, 3)),
            dma((pieces,)), dma((pieces,)),
            dma((n_dp,)), dma((n_dp,)),
            dma((TICKS, n_section)), dma((TICKS,)),
            dma((TICKS, n_dp)), dma((TICKS, n_dp)),
        ],
        compiler_params=pltpu.CompilerParams(
            collective_id=0, has_side_effects=True, vmem_limit_bytes=48 * 2**20
        ),
    )(
        w_query, w_key, w_value, w_out, norm_gain, saved_input, saved_query, saved_key,
        saved_value, grad_in, fresh_grad, features, image_pos,
    )
    total = lax.dot_general(
        feat_all.reshape(-1, own_rows),
        picks.reshape(-1, width),
        FIRST,
        preferred_element_type=jnp.float32,
    )
    return total.astype(bf16), pending


def solution(mesh):
    in_specs = (
        P("section", None, "mp"),
        P("section", None, "mp"),
        P("section", None, "mp"),
        P("section", "mp", None),
        P("section", "mp"),
        P("section", None, "dp", None, "mp"),
        P("section", None, "dp", None, "mp"),
        P("section", None, "dp", None, "mp"),
        P("section", None, "dp", None, "mp"),
        P("section", "dp", None, "mp"),
        P(None, "dp", None, "mp"),
        P(None, "dp", None, "section"),
        P(None, "dp", None),
    )
    out_specs = (P(("section", "dp"), "mp"), P("section", "dp", None, "mp"))
    return jax.shard_map(shards, mesh=mesh, in_specs=in_specs, out_specs=out_specs, check_vma=False)
```

```python
import functools

import jax
import jax.numpy as jnp
from jax import lax
from jax.experimental import pallas as pl
from jax.experimental.pallas import tpu as pltpu
from jax.sharding import PartitionSpec as P

HD = 128
LANES = 128
TICKS = 2
GAIN_ROWS = 16
MESH = pl.DeviceIdType.MESH
LAST = (((1,), (1,)), ((), ()))
FIRST = (((0,), (0,)), ((), ()))
PLAIN = (((1,), (0,)), ((), ()))


def mul(a, b, dims):
    return lax.dot_general(a, b, dims, preferred_element_type=jnp.float32)


def lane_sum(a):
    parts = [a[:, i : i + LANES] for i in range(0, a.shape[1], LANES)]
    return functools.reduce(lambda p, q: p + q, parts)


def kernel(
    n_section, n_dp, n_mp, pieces, halves,
    wq, wk, wv, wo, gain, x, q, k, v, g_in, fresh, feat, pos,
    feat_all, picks, pending,
    wq_s, wk_s, wv_s, wo_s, gain_s, x_s, q_s, k_s, v_s, g_s, feat_s, cut_s, pos_s,
    probs_s, attn_s, dq_s, dk_s, dv_s, out_s, send_s, recv_s, term_s, cross_s, cross_r,
    load_sem, wo_sem, wq_sem, wk_sem, wv_sem,
    ag_send, ag_recv, xg_send, xg_recv, rs_send, rs_recv, cr_send, cr_recv,
    held_send, held_recv, ft_send, ft_recv, px_send, px_recv, pz_send, pz_recv,
):
    section = lax.axis_index("section")
    seq = lax.axis_index("dp")
    me = lax.axis_index("mp")
    y, core = me // 2, me % 2
    partner = 2 * y + (1 - core)
    across = 2 * (1 - y) + core
    diag = 2 * (1 - y) + (1 - core)
    length = g_in.shape[2]
    width = g_in.shape[3]
    depth = width * n_mp
    kv_local = k.shape[4] // HD
    group = q.shape[4] // k.shape[4]
    scale = HD ** (-0.5)
    f32, bf16 = jnp.float32, jnp.bfloat16

    def remote(src, dst, ssem, rsem, where):
        return pltpu.make_async_remote_copy(
            src_ref=src, dst_ref=dst, send_sem=ssem, recv_sem=rsem,
            device_id=where, device_id_type=MESH,
        )

    loads = {}

    def load(name, src, dst, sem):
        loads[name] = pltpu.make_async_copy(src, dst, sem)
        loads[name].start()

    load("g", g_in.at[0, 0], g_s.at[0, me], load_sem.at[0])
    load("x0", x.at[0, 0, 0], x_s.at[0, me, pl.ds(0, length)], load_sem.at[1])
    load("gain", gain, gain_s, load_sem.at[2])
    load("x1", x.at[0, 1, 0], x_s.at[1, me, pl.ds(0, length)], load_sem.at[3])
    load("q", q.at[0, :, 0], q_s, load_sem.at[4])
    load("k", k.at[0, :, 0], k_s, load_sem.at[5])
    load("v", v.at[0, :, 0], v_s, load_sem.at[6])
    load("feat", feat.at[:, 0], feat_s, load_sem.at[7])
    load("pos", pos.at[:, 0], pos_s, load_sem.at[8])
    order = (me, partner, across, diag)
    for i, b in enumerate(order):
        columns = pl.ds(pl.multiple_of(b * width, width), width)
        load(f"wo{i}", wo.at[0, :, columns], wo_s.at[b], wo_sem.at[i])
    for i, b in enumerate((diag, across, partner, me)):
        rows = pl.ds(pl.multiple_of(b * width, width), width)
        load(f"wk{i}", wk.at[0, rows], wk_s.at[b], wk_sem.at[i])
        load(f"wv{i}", wv.at[0, rows], wv_s.at[b], wv_sem.at[i])
        load(f"wq{i}", wq.at[0, rows], wq_s.at[b], wq_sem.at[i])

    barrier = pltpu.get_barrier_semaphore()
    for b in (partner, across, diag):
        pl.semaphore_signal(barrier, inc=1, device_id={"mp": b}, device_id_type=MESH)
    for o in range(1, n_dp):
        pl.semaphore_signal(
            barrier, inc=1, device_id={"dp": (seq + o) % n_dp}, device_id_type=MESH
        )
    for o in range(1, n_section):
        pl.semaphore_signal(
            barrier, inc=1, device_id={"section": (section + o) % n_section}, device_id_type=MESH
        )
    pl.semaphore_wait(barrier, 3 + n_dp - 1 + n_section - 1)

    def gather_copy(buf, slot, rows, ssem, rsem, where):
        ref = buf.at[slot, rows]
        return remote(ref, ref, ssem, rsem, {"mp": where})

    def gather_start(buf, rows, ssem, rsem):
        gather_copy(buf, me, rows, ssem.at[1], rsem.at[1], across).start()
        gather_copy(buf, me, rows, ssem.at[0], rsem.at[0], partner).start()

    def gather_forward(buf, rows, ssem, rsem):
        gather_copy(buf, across, rows, ssem.at[1], rsem.at[1], across).wait_recv()
        gather_copy(buf, across, rows, ssem.at[2], rsem.at[2], partner).start()

    def gather_wait(buf, slot, which, rows, ssem, rsem):
        gather_copy(buf, slot, rows, ssem.at[which], rsem.at[which], partner).wait_recv()

    def gather_drain(buf, rows, ssem, rsem):
        for i in range(3):
            gather_copy(buf, me, rows, ssem.at[i], rsem.at[i], partner).wait_send()

    full = pl.ds(0, length)
    x_rows = (pl.ds(0, length + GAIN_ROWS), pl.ds(0, length))
    loads["g"].wait()
    gather_start(g_s.at[0], full, ag_send.at[0, 0], ag_recv.at[0, 0])
    loads["x0"].wait()
    loads["gain"].wait()
    x_s[0, me, pl.ds(length, GAIN_ROWS), :] = jnp.broadcast_to(
        gain_s[...], (GAIN_ROWS, width)
    )
    gather_start(x_s.at[0], x_rows[0], xg_send.at[0], xg_recv.at[0])
    loads["x1"].wait()
    gather_start(x_s.at[1], x_rows[1], xg_send.at[1], xg_recv.at[1])

    loads["feat"].wait()
    own_rows = feat_s.shape[2] // n_dp
    for j in range(n_dp):
        for t in range(TICKS):
            cut_s[j, pl.ds(t * feat_s.shape[1], feat_s.shape[1]), :] = feat_s[
                t, :, j * own_rows : (j + 1) * own_rows
            ]
    feat_own = pltpu.make_async_copy(cut_s.at[seq], feat_all.at[seq], load_sem.at[9])
    feat_own.start()

    def feat_copy(o):
        to = (seq + o) % n_dp
        return remote(
            cut_s.at[to], feat_all.at[seq], ft_send.at[o], ft_recv.at[o], {"dp": to}
        )

    for o in range(1, n_dp):
        feat_copy(o).start()

    loads["q"].wait()
    loads["k"].wait()
    loads["v"].wait()

    def stack(a, g):
        return jnp.concatenate(
            [a[:, (g * group + j) * HD : (g * group + j + 1) * HD] for j in range(group)], axis=0
        )

    rows_at = lax.rem(
        lax.broadcasted_iota(jnp.int32, (group * length, length), 0), jnp.int32(length)
    )
    cols_at = lax.broadcasted_iota(jnp.int32, (group * length, length), 1)
    causal = cols_at <= rows_at

    def softmax(t):
        for g in range(kv_local):
            kg = k_s[t, :, g * HD : (g + 1) * HD]
            scores = mul(stack(q_s[t], g), kg, LAST) * scale
            scores = jnp.where(causal, scores, -1e30)
            expo = jnp.exp(scores - jnp.max(scores, -1, keepdims=True))
            probs_s[t, g] = expo / jnp.sum(expo, -1, keepdims=True)

    for t in range(TICKS):
        softmax(t)

    def picks_second(t):
        @pl.when(section > 0)
        def _():
            remote(
                picks.at[seq, t], picks.at[seq, t], px_send.at[t, 0], px_recv.at[t],
                {"section": section},
            ).wait_recv()

        for o in range(1, n_dp):
            pick_copy(t, o).start()

    def pick_copy(t, o):
        to = (seq + o) % n_dp
        ref = picks.at[seq, t]
        return remote(ref, ref, pz_send.at[t, o], pz_recv.at[t, o], {"dp": to})

    def pick_spread(t, o):
        ref = picks.at[seq, t]
        return remote(ref, ref, px_send.at[t, o], px_recv.at[t], {"section": o})

    block = width // halves

    def rs_copy(t, i, h, where):
        lanes = pl.ds(h * block, block)
        return remote(
            send_s.at[t, i, :, lanes], recv_s.at[t, i, :, lanes],
            rs_send.at[t, i, h], rs_recv.at[t, i, h], {"mp": where},
        )

    def cross_copy(t, i, where):
        return remote(
            cross_s.at[t], cross_r.at[t, i], cr_send.at[t, i], cr_recv.at[t, i], {"mp": where}
        )

    part = length // pieces

    def held_copy(h):
        rows = pl.ds(h * part, part)
        return remote(
            out_s.at[0, rows], g_s.at[1, me, rows], held_send.at[h], held_recv.at[h],
            {"section": section - 1},
        )

    def finish_gather(t, rows_list):
        for h, rows in enumerate(rows_list):
            gather_forward(g_s.at[t], rows, ag_send.at[t, h], ag_recv.at[t, h])

    def tick(t):
        rows_list = [full] if t == 0 else [pl.ds(h * part, part) for h in range(pieces)]
        first = t == 0
        if t == 1:

            @pl.when(section == n_section - 1)
            def _():
                fresh_copy = pltpu.make_async_copy(
                    fresh.at[0, 0], g_s.at[1, me], load_sem.at[10]
                )
                fresh_copy.start()
                fresh_copy.wait()

            for h, rows in enumerate(rows_list):

                @pl.when(section < n_section - 1)
                def _():
                    held_copy(h).wait_recv()

                gather_start(g_s.at[1], rows, ag_send.at[1, h], ag_recv.at[1, h])
        if first:
            loads["wo0"].wait()
        d_attn = mul(g_s[t, me], wo_s[me], LAST)
        for h, rows in enumerate(rows_list):
            gather_wait(g_s.at[t], partner, 0, rows, ag_send.at[t, h], ag_recv.at[t, h])
        if first:
            loads["wo1"].wait()
        d_attn += mul(g_s[t, partner], wo_s[partner], LAST)
        finish_gather(t, rows_list)
        if first:
            loads["wo2"].wait()
        d_attn += mul(g_s[t, across], wo_s[across], LAST)
        for h, rows in enumerate(rows_list):
            gather_wait(g_s.at[t], diag, 2, rows, ag_send.at[t, h], ag_recv.at[t, h])
        if first:
            loads["wo3"].wait()
        d_attn += mul(g_s[t, diag], wo_s[diag], LAST)
        attn_s[...] = d_attn.astype(bf16)
        if not first:
            picks_second(0)

        for g in range(kv_local):
            lanes = slice(g * HD, (g + 1) * HD)
            kg, vg = k_s[t, :, lanes], v_s[t, :, lanes]
            qg = stack(q_s[t], g)
            ag = stack(attn_s[...], g)
            probs = probs_s[t, g]
            d_probs = mul(ag, vg, LAST)
            inner = jnp.sum(probs * d_probs, -1, keepdims=True)
            d_scores = (probs * (d_probs - inner) * scale).astype(bf16)
            d_query = mul(d_scores, kg, PLAIN).astype(bf16)
            for j in range(group):
                dq_s[:, (g * group + j) * HD : (g * group + j + 1) * HD] = d_query[
                    j * length : (j + 1) * length
                ]
            dk_s[:, lanes] = mul(d_scores, qg, FIRST).astype(bf16)
            dv_s[:, lanes] = mul(probs.astype(bf16), ag, FIRST).astype(bf16)

        def x_of(b):
            return x_s[t, b, pl.ds(0, length), :].astype(f32)

        def gain_of(b):
            return x_s[0, b, pl.ds(length, GAIN_ROWS), :].astype(f32)[0:1]

        def partial(i, b, h):
            if first and h == 0:
                loads[f"wk{i}"].wait()
                loads[f"wv{i}"].wait()
                loads[f"wq{i}"].wait()
            at = slice(h * block, (h + 1) * block)
            term = mul(dq_s[...], wq_s[b, at], LAST)
            term += mul(dk_s[...], wk_s[b, at], LAST)
            term += mul(dv_s[...], wv_s[b, at], LAST)
            term_s[i, :, at] = term
            return at, term

        for h in range(halves):
            at, term = partial(0, diag, h)
            send_s[t, 0, :, at] = term.astype(bf16)
            rs_copy(t, 0, h, partner).start()
        for h in range(halves):
            at, term = partial(1, across, h)
            rs_copy(t, 0, h, partner).wait_recv()
            send_s[t, 1, :, at] = (term + recv_s[t, 0, :, at].astype(f32)).astype(bf16)
            rs_copy(t, 1, h, across).start()
        for h in range(halves):
            at, term = partial(2, partner, h)
            send_s[t, 2, :, at] = term.astype(bf16)
            rs_copy(t, 2, h, partner).start()
        if first:
            gather_forward(x_s.at[0], x_rows[0], xg_send.at[0], xg_recv.at[0])
        for h in range(halves):
            partial(3, me, h)
        gather_wait(x_s.at[t], partner, 0, x_rows[t], xg_send.at[t], xg_recv.at[t])
        total = jnp.zeros((length, LANES), f32)
        for i, b in ((1, across), (2, partner), (3, me), (0, diag)):
            if i == 0:
                gather_wait(x_s.at[t], diag, 2, x_rows[t], xg_send.at[t], xg_recv.at[t])
            total += lane_sum(x_of(b) * gain_of(b) * term_s[i])
        padded = jnp.concatenate([total, jnp.zeros((LANES - length, LANES), f32)], axis=0)
        cross_s[t] = jnp.broadcast_to(
            jnp.sum(padded.T, axis=0, keepdims=True), cross_s.shape[1:]
        )
        for i, b in enumerate((partner, across, diag)):
            cross_copy(t, i, b).start()
        if first:
            gather_forward(x_s.at[1], x_rows[1], xg_send.at[1], xg_recv.at[1])
        squares = functools.reduce(
            lambda a, b: a + b, [lane_sum(x_of(b) * x_of(b)) for b in range(n_mp)]
        )
        squares = jnp.sum(squares, -1, keepdims=True)
        rstd = lax.rsqrt(squares / depth + 1e-05)
        for h in range(halves):
            rs_copy(t, 2, h, partner).wait_recv()
        for h in range(halves):
            rs_copy(t, 1, h, across).wait_recv()
        cross = cross_s[t]
        for i in range(3):
            cross_copy(t, i, partner).wait_recv()
            cross += cross_r[t, i]
        cross = jnp.broadcast_to(cross[0:1], (LANES, LANES)).T[:length, 0:1]
        factor = rstd * rstd * rstd * (cross / depth)
        for h in range(pieces if first else 1):
            rows = slice(h * part, (h + 1) * part) if first else slice(0, length)
            d_normed = (
                term_s[3, rows] + recv_s[t, 2, rows].astype(f32) + recv_s[t, 1, rows].astype(f32)
            )
            own = x_s[t, me, rows].astype(f32)
            d_input = rstd[rows] * (gain_of(me) * d_normed) - own * factor[rows]
            out_s[t, rows] = (g_s[t, me, rows].astype(f32) + d_input).astype(bf16)
            if first:

                @pl.when(section > 0)
                def _():
                    held_copy(h).start()

        if first:
            loads["pos"].wait()

        @pl.when(section == 0)
        def _():
            at = lax.broadcasted_iota(jnp.int32, (length, pos_s.shape[1]), 0)
            chosen = (at == pos_s[pl.ds(t, 1), :]).astype(f32).astype(bf16)
            picks[seq, t] = mul(chosen, out_s[t], FIRST).astype(bf16)
            for o in range(1, n_section):
                pick_spread(t, o).start()

    tick(0)
    tick(1)
    picks_second(1)
    pending[0, 0] = out_s[1]

    feat_own.wait()
    gather_drain(g_s.at[0], full, ag_send.at[0, 0], ag_recv.at[0, 0])
    for h in range(pieces):
        gather_drain(
            g_s.at[1], pl.ds(h * part, part), ag_send.at[1, h], ag_recv.at[1, h]
        )
    for t in range(TICKS):
        gather_drain(x_s.at[t], x_rows[t], xg_send.at[t], xg_recv.at[t])
        for i in range(3):
            for h in range(halves):
                rs_copy(t, i, h, partner).wait_send()
            cross_copy(t, i, partner).wait_send()

    @pl.when(section > 0)
    def _():
        for h in range(pieces):
            held_copy(h).wait_send()

    @pl.when(section == 0)
    def _():
        for t in range(TICKS):
            for o in range(1, n_section):
                pick_spread(t, o).wait_send()

    for o in range(1, n_dp):
        feat_copy(o).wait_send()
        source = (seq + n_dp - o) % n_dp
        remote(
            cut_s.at[seq], feat_all.at[source], ft_send.at[o], ft_recv.at[o], {"dp": source}
        ).wait_recv()
        for t in range(TICKS):
            pick_copy(t, o).wait_send()
            ref = picks.at[source, t]
            remote(ref, ref, pz_send.at[t, o], pz_recv.at[t, o], {"dp": source}).wait_recv()


def shards(
    w_query, w_key, w_value, w_out, norm_gain, saved_input, saved_query, saved_key,
    saved_value, grad_in, fresh_grad, features, image_pos, pieces=4, halves=1,
):
    n_section, n_dp, n_mp = (lax.axis_size(a) for a in ("section", "dp", "mp"))
    assert n_mp == 4
    length, width = grad_in.shape[2:]
    kw = saved_key.shape[4]
    kv_local = kw // HD
    group = width // kw
    images = features.shape[2]
    own_rows = features.shape[3] // n_dp
    f32, bf16 = jnp.float32, jnp.bfloat16
    vmem, dma = pltpu.VMEM, pltpu.SemaphoreType.DMA
    feat_all, picks, pending = pl.pallas_call(
        functools.partial(kernel, n_section, n_dp, n_mp, pieces, halves),
        out_shape=(
            jax.ShapeDtypeStruct((n_dp, TICKS * images, own_rows), bf16),
            jax.ShapeDtypeStruct((n_dp, TICKS, images, width), bf16),
            jax.ShapeDtypeStruct((1, 1, length, width), bf16),
        ),
        in_specs=[pl.BlockSpec(memory_space=pltpu.HBM)] * 13,
        out_specs=(pl.BlockSpec(memory_space=pltpu.VMEM),) * 3,
        scratch_shapes=[
            vmem((n_mp, width, width), bf16),
            vmem((n_mp, width, kw), bf16),
            vmem((n_mp, width, kw), bf16),
            vmem((n_mp, width, width), bf16),
            vmem((1, width), bf16),
            vmem((TICKS, n_mp, length + GAIN_ROWS, width), bf16),
            vmem((TICKS, length, width), bf16),
            vmem((TICKS, length, kw), bf16),
            vmem((TICKS, length, kw), bf16),
            vmem((TICKS, n_mp, length, width), bf16),
            vmem((TICKS, images, features.shape[3]), bf16),
            vmem((n_dp, TICKS * images, own_rows), bf16),
            vmem((TICKS, images), jnp.int32),
            vmem((TICKS, kv_local, group * length, length), f32),
            vmem((length, width), bf16),
            vmem((length, width), bf16),
            vmem((length, kw), bf16),
            vmem((length, kw), bf16),
            vmem((TICKS, length, width), bf16),
            vmem((TICKS, 3, length, width), bf16),
            vmem((TICKS, 3, length, width), bf16),
            vmem((n_mp, length, width), f32),
            vmem((TICKS, 8, LANES), f32),
            vmem((TICKS, 3, 8, LANES), f32),
            dma((11,)), dma((n_mp,)), dma((n_mp,)), dma((n_mp,)), dma((n_mp,)),
            dma((TICKS, pieces, 3)), dma((TICKS, pieces, 3)),
            dma((TICKS, 3)), dma((TICKS, 3)),
            dma((TICKS, 3, halves)), dma((TICKS, 3, halves)), dma((TICKS, 3)), dma((TICKS, 3)),
            dma((pieces,)), dma((pieces,)),
            dma((n_dp,)), dma((n_dp,)),
            dma((TICKS, n_section)), dma((TICKS,)),
            dma((TICKS, n_dp)), dma((TICKS, n_dp)),
        ],
        compiler_params=pltpu.CompilerParams(
            collective_id=0, has_side_effects=True, vmem_limit_bytes=48 * 2**20
        ),
    )(
        *[
            pltpu.with_memory_space_constraint(a, pltpu.HBM)
            for a in (
                w_query, w_key, w_value, w_out, norm_gain, saved_input, saved_query, saved_key,
                saved_value, grad_in, fresh_grad, features, image_pos,
            )
        ]
    )
    total = lax.dot_general(
        feat_all.reshape(-1, own_rows),
        picks.reshape(-1, width),
        FIRST,
        preferred_element_type=jnp.float32,
    )
    return total.astype(bf16), pending


def solution(mesh):
    in_specs = (
        P("section", None, "mp"),
        P("section", None, "mp"),
        P("section", None, "mp"),
        P("section", "mp", None),
        P("section", "mp"),
        P("section", None, "dp", None, "mp"),
        P("section", None, "dp", None, "mp"),
        P("section", None, "dp", None, "mp"),
        P("section", None, "dp", None, "mp"),
        P("section", "dp", None, "mp"),
        P(None, "dp", None, "mp"),
        P(None, "dp", None, "section"),
        P(None, "dp", None),
    )
    out_specs = (P(("section", "dp"), "mp"), P("section", "dp", None, "mp"))
    return jax.shard_map(shards, mesh=mesh, in_specs=in_specs, out_specs=out_specs, check_vma=False)
```
